512 devices in a mesh: dp: 2 (over z_lo), ctx: 64 (over y, x, core), tp: 4 (over z_hi).
Axes of the slice: x: 4, y: 8, z: 8 (z_hi: 4, z_lo: 2; z = z_hi * 2 + z_lo), core: 2. Of those that a mesh axis runs over, the one named last changes fastest.
Arguments:
- queries: bfloat16 [65536, 4096], P(('dp', 'ctx'), 'tp'), parts along dimension 0, may hold values from -6 to 6
- keys: bfloat16 [65536, 4096], P(('dp', 'ctx'), 'tp'), parts along dimension 0, may hold values from -6 to 6
- values: bfloat16 [65536, 4096], P(('dp', 'ctx'), 'tp'), parts along dimension 0, may hold values from -6 to 6
Outputs:
- attended: bfloat16 [65536, 4096], P(('dp', 'ctx'), 'tp'), parts along dimension 0
The draws below stay inside these ranges and needn't reach their ends.
There are 2 independent parts, one for each index of `dp`. The reference program is written for one: setup_inputs(seed, part) draws one part's arguments, and reference() takes and returns one part's arrays. A program takes and returns all parts, laid end to end along the dimension named above; each array names one. Nothing has to cross between parts.
All inputs are finite; a program needn't handle non-finite values.
Results may differ from the reference program's by a relative error of at most 0.0069.
Values may be sent and summed in bfloat16 or wider, within the bound.
A program may use at most 64 MiB of HBM per device.

```python
import jax
import jax.numpy as jnp
from jax import lax

HEADS = 32
HEAD_DIM = 128
BLOCK = 128
LEN = 32768


def draw_queries(key, part):
    col_count = HEADS * HEAD_DIM
    base_key = jax.random.fold_in(key, 101)
    dense = 1.2 * jax.random.normal(base_key, (LEN, col_count), jnp.float32)
    return jnp.clip(dense, -6.0, 6.0).astype(jnp.bfloat16)


def draw_keys(key, part):
    col_count = HEADS * HEAD_DIM
    base_key = jax.random.fold_in(key, 202)
    noise_key = jax.random.fold_in(base_key, 1)
    block_key = jax.random.fold_in(base_key, 2)
    noise = jax.random.normal(noise_key, (LEN, col_count), jnp.float32)
    regional = 1.2 * jax.random.normal(block_key, (LEN // BLOCK, col_count), jnp.float32)
    dense = noise + jnp.repeat(regional, BLOCK, axis=0)
    return jnp.clip(dense, -6.0, 6.0).astype(jnp.bfloat16)


def draw_values(key, part):
    col_count = HEADS * HEAD_DIM
    base_key = jax.random.fold_in(key, 303)
    noise_key = jax.random.fold_in(base_key, 1)
    block_key = jax.random.fold_in(base_key, 2)
    noise = jax.random.normal(noise_key, (LEN, col_count), jnp.float32)
    regional = jax.random.normal(block_key, (LEN // BLOCK, col_count), jnp.float32)
    dense = noise + jnp.repeat(regional, BLOCK, axis=0)
    return jnp.clip(dense, -6.0, 6.0).astype(jnp.bfloat16)


def setup_inputs(seed: int = 0, part: int = 0) -> dict:
    seeds = jax.random.split(jax.random.key(seed), 4)
    part_keys = jax.random.split(jax.random.fold_in(seeds[3], part), 4)
    queries = draw_queries(jax.random.fold_in(jax.random.fold_in(seeds[3], part), 71), part)
    keys = draw_keys(jax.random.fold_in(jax.random.fold_in(seeds[3], part), 71), part)
    values = draw_values(jax.random.fold_in(jax.random.fold_in(seeds[3], part), 71), part)
    return dict(queries=queries, keys=keys, values=values)


masked_score = -1.0e30


def pair_mean(source):
    source_shape = source.shape
    paired = source.reshape(source_shape[:-2] + (source_shape[-2] // 2, 2, source_shape[-1])).astype(jnp.float32)
    return ((paired[..., 0, :] + paired[..., 1, :]) * 0.5).astype(jnp.bfloat16)


def sibling_blocks(coarse, height, block_rows):
    row_count = coarse.shape[1]
    head_dim = coarse.shape[2]
    groups = coarse.reshape(2, row_count // (2 * block_rows), 2, block_rows, head_dim)[:, :, ::-1]
    swapped = groups.reshape(2, row_count // block_rows, block_rows, head_dim)
    return jnp.repeat(swapped, 2 ** height, axis=1)


def attend(query_tiles_grouped, key_tiles_grouped, value_tiles_grouped, usable):
    logit_scale_factor = 1.0 / (query_tiles_grouped.shape[-1] ** 0.5)
    logit_matrix = jnp.einsum("sac,sec->sae", query_tiles_grouped.astype(jnp.float32), key_tiles_grouped.astype(jnp.float32)) * logit_scale_factor
    logit_matrix = jnp.where(usable[:, None, :], logit_matrix, masked_score)
    row_peak = jnp.max(logit_matrix, axis=-1, keepdims=True)
    weights = jnp.exp(logit_matrix - row_peak)
    row_total = jnp.sum(weights, axis=-1, keepdims=True)
    rounded_scores = lax.optimization_barrier(weights.astype(jnp.bfloat16))
    weighted_value_sum = jnp.einsum("zif,zfo->zio", rounded_scores.astype(jnp.float32), value_tiles_grouped.astype(jnp.float32))
    return (weighted_value_sum / row_total).astype(jnp.bfloat16)


def reference(queries, keys, values):
    length, width = queries.shape
    heads = HEADS
    head_dim = width // heads
    block_rows = BLOCK
    blocks = length // block_rows
    top_level = blocks.bit_length() - 2
    starts = jnp.arange(blocks, dtype=jnp.int32) * block_rows
    position = starts[:, None] + jnp.arange(3 * block_rows, dtype=jnp.int32)[None, :] - block_rows
    fine_usable = (position >= 0) & (position < length)
    usable = jnp.concatenate([fine_usable, jnp.ones((blocks, top_level * block_rows), bool)], axis=1)

    def one_head(head):
        def columns(source):
            return lax.dynamic_slice_in_dim(source, head * head_dim, head_dim, 1)
        query_part = columns(queries)
        stacked = jnp.stack([columns(keys), columns(values)])
        padded = jnp.pad(stacked, ((0, 0), (block_rows, block_rows), (0, 0)))
        key_parts = [jnp.concatenate([padded[:, offset * block_rows:offset * block_rows + length].reshape(2, blocks, block_rows, head_dim) for offset in range(3)], axis=2)]
        coarse = stacked
        for height in range(1, top_level + 1):
            coarse = pair_mean(coarse)
            key_parts.append(sibling_blocks(coarse, height, block_rows))
        key_value = jnp.concatenate(key_parts, axis=2)
        result = attend(query_part.reshape(blocks, block_rows, head_dim), key_value[0], key_value[1], usable)
        return result.reshape(length, head_dim)

    head_outputs = lax.map(one_head, jnp.arange(heads, dtype=jnp.int32))
    return jnp.transpose(head_outputs, (1, 0, 2)).reshape(length, width)
```

```python
import functools
import math

import jax
import jax.numpy as jnp
from jax import lax
from jax.experimental import pallas as pl
from jax.experimental.pallas import tpu as pltpu
from jax.sharding import PartitionSpec as P

HEAD_DIM = 128
BLOCK = 128
ROWS = 512
CTX = 64
PACK = 48
MASKED = -1.0e30
LOG2E = 1.4426950408889634

F32 = jnp.float32
BF16 = jnp.bfloat16

HALO = 0
LEVEL2 = 4
LEVEL3 = 5
LEVEL4 = 6
LEVEL5 = 8
LEVEL6 = 9
LEVEL7 = 11
ALONG_X = 15
HALF34 = 18
SHARE = 19
COPIES = 23


def flip(place, mask):
    bit = 1
    while bit <= mask:
        if mask & bit:
            place = place + bit * (1 - 2 * lax.rem(lax.div(place, bit), 2))
        bit *= 2
    return place


def averaging(rows, cols):
    row = lax.broadcasted_iota(jnp.int32, (rows, cols), 0)
    col = lax.broadcasted_iota(jnp.int32, (rows, cols), 1)
    hit = (col == 2 * row) | (col == 2 * row + 1)
    return jnp.where(hit, 0.5, 0.0).astype(BF16)


def pair_mean(source, rows=None):
    rows = source.shape[0] // 2 if rows is None else rows
    weights = averaging(rows, source.shape[0])
    return jnp.dot(weights, source, preferred_element_type=F32).astype(BF16)


def kernel(
    q_ref, k_ref, v_ref, o_ref,
    halo, c1, c2, c3, c4, c5, c6, c7, far2, far34, got6, got7, far567,
    acc, peak, total, send_sem, recv_sem,
):
    heads = q_ref.shape[1] // HEAD_DIM
    scale = LOG2E / math.sqrt(HEAD_DIM)
    me = lax.axis_index("ctx")
    core = lax.rem(me, 2)
    x = lax.rem(lax.div(me, 2), 4)
    up = lax.rem(me + 1, CTX)
    down = lax.rem(me + CTX - 1, CTX)

    barrier = pltpu.get_barrier_semaphore()
    peers = [up, down] + [flip(me, mask) for mask in (1, 2, 4, 6, 8, 16, 24, 32, 40, 48, 56)]
    for peer in peers:
        pl.semaphore_signal(
            barrier, inc=1, device_id={"ctx": peer}, device_id_type=pl.DeviceIdType.MESH
        )

    def copy(number, source, target, device):
        return pltpu.make_async_remote_copy(
            src_ref=source,
            dst_ref=target,
            send_sem=send_sem.at[number],
            recv_sem=recv_sem.at[number],
            device_id={"ctx": device},
            device_id_type=pl.DeviceIdType.MESH,
        )

    for which, ref in ((0, k_ref), (1, v_ref)):
        for half in range(2):
            c1[which, half * 128:(half + 1) * 128] = pair_mean(ref[half * 256:(half + 1) * 256])
        c2[which] = pair_mean(c1[which])
        c3[which] = pair_mean(c2[which])
        c4[which] = pair_mean(c3[which])
        c5[which] = pair_mean(c4[which])
    c6[...] = pair_mean(c5[...].reshape(32, c5.shape[2]))
    c7[...] = pair_mean(c6[...], 16)

    pl.semaphore_wait(barrier, len(peers))

    copies = {}
    copies[LEVEL5] = copy(LEVEL5, c5, far567.at[:, core, x, pl.ds(0, 16)], flip(me, 8))
    for j in range(2):
        copies[LEVEL6 + j] = copy(LEVEL6 + j, c6, got6.at[j], flip(me, 16 + 8 * j))
    for j in range(4):
        copies[LEVEL7 + j] = copy(LEVEL7 + j, c7, got7.at[j], flip(me, 32 + 8 * j))
    last, first = pl.ds(ROWS - BLOCK, BLOCK), pl.ds(0, BLOCK)
    copies[HALO] = copy(HALO, k_ref.at[last], halo.at[0, 0], up)
    copies[HALO + 1] = copy(HALO + 1, v_ref.at[last], halo.at[1, 0], up)
    copies[HALO + 2] = copy(HALO + 2, k_ref.at[first], halo.at[0, 1], down)
    copies[HALO + 3] = copy(HALO + 3, v_ref.at[first], halo.at[1, 1], down)
    copies[LEVEL2] = copy(LEVEL2, c2, far2, flip(me, 1))
    copies[LEVEL3] = copy(LEVEL3, c3, far34.at[:, core, pl.ds(0, 64)], flip(me, 2))
    for j in range(2):
        copies[LEVEL4 + j] = copy(
            LEVEL4 + j, c4, far34.at[:, core, pl.ds(64 + 32 * j, 32)], flip(me, 4 + 2 * j)
        )
    for item in copies.values():
        item.start()

    def attend(head, row, rows, keys, values, first=False, last=False, valid=None):
        lanes = pl.ds(pl.multiple_of(head * HEAD_DIM, HEAD_DIM), HEAD_DIM)
        span = pl.ds(row, rows)
        count = keys.shape[0]
        scores = lax.dot_general(
            q_ref[span, lanes], keys, (((1,), (1,)), ((), ())), preferred_element_type=F32
        )
        if valid is not None:
            edge = jnp.where(valid, scores[:, :BLOCK], MASKED)
            scores = jnp.concatenate([edge, scores[:, BLOCK:]], axis=1)
        top = jnp.max(scores, axis=1, keepdims=True)
        if first:
            new = jnp.broadcast_to(top, (rows, 128))
        else:
            old = peak[head, span]
            new = jnp.maximum(old, top)
            fade = jnp.exp2((old - new) * scale)
        wide = jnp.concatenate([new] * (count // 128), axis=1)
        weights = jnp.exp2((scores - wide) * scale).astype(BF16)
        ones = jnp.ones((count, 128), BF16)
        both = jnp.dot(
            weights, jnp.concatenate([values, ones], axis=1), preferred_element_type=F32
        )
        part, part_total = both[:, :128], both[:, 128:]
        if not first:
            part = acc[head, span] * fade + part
            part_total = total[head, span] * fade + part_total
        if last:
            o_ref[span, lanes] = (part / part_total).astype(BF16)
        else:
            acc[head, span] = part
            total[head, span] = part_total
            peak[head, span] = new

    def lanes_of(head):
        return pl.ds(pl.multiple_of(head * HEAD_DIM, HEAD_DIM), HEAD_DIM)

    def own(head, carry):
        lanes = lanes_of(head)
        for block in range(4):
            low, high = max(block - 1, 0) * BLOCK, min(block + 2, 4) * BLOCK
            side = pl.ds(128 if block < 2 else 0, 128)
            keys = jnp.concatenate([k_ref[low:high, lanes], c1[0, side, lanes]], axis=0)
            values = jnp.concatenate([v_ref[low:high, lanes], c1[1, side, lanes]], axis=0)
            attend(head, block * BLOCK, BLOCK, keys, values, first=True)
        return carry

    lax.fori_loop(0, heads, own, 0)

    for number in range(LEVEL5, LEVEL7 + 4):
        copies[number].wait_recv()
    for which in range(2):
        rows6 = [got6[j, 8 * which:8 * which + 8].astype(F32) for j in range(2)]
        rows7 = [got7[j, 0:8].astype(F32)[4 * which:4 * which + 4] for j in range(4)]
        far567[which, core, x, 16:32] = jnp.concatenate(rows6, axis=0).astype(BF16)
        far567[which, core, x, 32:48] = jnp.concatenate(rows7, axis=0).astype(BF16)
    mine = far567.at[:, core, x]
    for j in range(1, 4):
        copies[ALONG_X + j - 1] = copy(ALONG_X + j - 1, mine, mine, flip(me, 2 * j))
        copies[ALONG_X + j - 1].start()
    copies[SHARE] = copy(SHARE, mine, mine, flip(me, 1))
    copies[SHARE].start()

    for number in (LEVEL3, LEVEL4, LEVEL4 + 1):
        copies[number].wait_recv()
    half = far34.at[:, core]
    copies[HALF34] = copy(HALF34, half, half, flip(me, 1))
    copies[HALF34].start()

    for number in range(HALO, LEVEL2 + 1):
        copies[number].wait_recv()

    def near(head, carry):
        lanes = lanes_of(head)
        keys2, values2 = far2[0, :, lanes], far2[1, :, lanes]
        for side, row, valid in ((0, 0, me > 0), (1, 3 * BLOCK, me < CTX - 1)):
            keys = jnp.concatenate([halo[0, side, :, lanes], keys2], axis=0)
            values = jnp.concatenate([halo[1, side, :, lanes], values2], axis=0)
            attend(head, row, BLOCK, keys, values, valid=valid)
        attend(head, BLOCK, 2 * BLOCK, keys2, values2)
        return carry

    lax.fori_loop(0, heads, near, 0)

    for j in range(1, 4):
        copies[ALONG_X + j - 1].wait_recv()
        came = far567.at[:, core, flip(x, j)]
        copies[SHARE + j] = copy(SHARE + j, came, came, flip(me, 1))
        copies[SHARE + j].start()

    copies[HALF34].wait_recv()

    def middle(head, carry):
        lanes = lanes_of(head)
        keys = far34[0, :, :, lanes].reshape(256, HEAD_DIM)
        values = far34[1, :, :, lanes].reshape(256, HEAD_DIM)
        for part in range(2):
            attend(head, part * 256, 256, keys, values)
        return carry

    lax.fori_loop(0, heads, middle, 0)

    for j in range(4):
        copies[SHARE + j].wait_recv()

    def distant(head, carry):
        lanes = lanes_of(head)
        keys = far567[0, :, :, :, lanes].reshape(8 * PACK, HEAD_DIM)
        values = far567[1, :, :, :, lanes].reshape(8 * PACK, HEAD_DIM)
        for part in range(2):
            attend(head, part * 256, 256, keys, values, last=True)
        return carry

    lax.fori_loop(0, heads, distant, 0)

    for item in copies.values():
        item.wait_send()


def per_device(queries, keys, values):
    rows, width = queries.shape
    heads = width // HEAD_DIM
    state = pltpu.VMEM((heads, rows, 128), F32)
    return pl.pallas_call(
        kernel,
        out_shape=jax.ShapeDtypeStruct((rows, width), BF16),
        in_specs=[pl.BlockSpec(memory_space=pltpu.VMEM)] * 3,
        out_specs=pl.BlockSpec(memory_space=pltpu.VMEM),
        scratch_shapes=[
            pltpu.VMEM((2, 2, BLOCK, width), BF16),
            pltpu.VMEM((2, 256, width), BF16),
            pltpu.VMEM((2, 128, width), BF16),
            pltpu.VMEM((2, 64, width), BF16),
            pltpu.VMEM((2, 32, width), BF16),
            pltpu.VMEM((2, 16, width), BF16),
            pltpu.VMEM((16, width), BF16),
            pltpu.VMEM((16, width), BF16),
            pltpu.VMEM((2, 128, width), BF16),
            pltpu.VMEM((2, 2, 128, width), BF16),
            pltpu.VMEM((2, 16, width), BF16),
            pltpu.VMEM((4, 16, width), BF16),
            pltpu.VMEM((2, 2, 4, PACK, width), BF16),
            state, state, state,
            pltpu.SemaphoreType.DMA((COPIES,)),
            pltpu.SemaphoreType.DMA((COPIES,)),
        ],
        compiler_params=pltpu.CompilerParams(
            collective_id=0, has_side_effects=True, vmem_limit_bytes=48 * 1024 * 1024
        ),
        name="hierarchical_attention",
    )(queries, keys, values)


def solution(mesh):
    return jax.shard_map(
        per_device,
        mesh=mesh,
        in_specs=(P(("dp", "ctx"), "tp"), P(("dp", "ctx"), "tp"), P(("dp", "ctx"), "tp")),
        out_specs=P(("dp", "ctx"), "tp"),
        check_vma=False,
    )
```

```python
import functools
import math

import jax
import jax.numpy as jnp
from jax import lax
from jax.experimental import pallas as pl
from jax.experimental.pallas import tpu as pltpu
from jax.sharding import PartitionSpec as P

HEAD_DIM = 128
BLOCK = 128
ROWS = 512
CTX = 64
PACK = 48
MASKED = -1.0e30
LOG2E = 1.4426950408889634

F32 = jnp.float32
BF16 = jnp.bfloat16

HALO = 0
LEVEL2 = 4
LEVEL3 = 5
LEVEL4 = 7
LEVEL5 = 9
LEVEL6 = 10
LEVEL7 = 12
ALONG_X = 16
SHARE4 = 19
SHARE3 = 21
SHARE = 22
COPIES = 26


def flip(place, mask):
    bit = 1
    while bit <= mask:
        if mask & bit:
            place = place + bit * (1 - 2 * lax.rem(lax.div(place, bit), 2))
        bit *= 2
    return place


def averaging(rows, cols):
    row = lax.broadcasted_iota(jnp.int32, (rows, cols), 0)
    col = lax.broadcasted_iota(jnp.int32, (rows, cols), 1)
    hit = (col == 2 * row) | (col == 2 * row + 1)
    return jnp.where(hit, 0.5, 0.0).astype(BF16)


def pair_mean(source, rows=None):
    rows = source.shape[0] // 2 if rows is None else rows
    weights = averaging(rows, source.shape[0])
    return jnp.dot(weights, source, preferred_element_type=F32).astype(BF16)


def kernel(
    q_hbm, k_hbm, v_hbm, o_ref, q_ref, k_ref, v_ref,
    halo, c1, c2, c3, c4, c5, c6, c7, far2, far3, far4, got6, got7, far567,
    acc, peak, total, send_sem, recv_sem, load_sem,
):
    heads = q_ref.shape[1] // HEAD_DIM
    scale = LOG2E / math.sqrt(HEAD_DIM)
    me = lax.axis_index("ctx")
    core = lax.rem(me, 2)
    x = lax.rem(lax.div(me, 2), 4)
    up = lax.rem(me + 1, CTX)
    down = lax.rem(me + CTX - 1, CTX)

    loads = [
        pltpu.make_async_copy(source, target, load_sem.at[number])
        for number, (source, target) in enumerate(((k_hbm, k_ref), (v_hbm, v_ref), (q_hbm, q_ref)))
    ]
    for load in loads:
        load.start()

    barrier = pltpu.get_barrier_semaphore()
    peers = [up, down] + [flip(me, mask) for mask in (1, 2, 4, 6, 8, 16, 24, 32, 40, 48, 56)]
    for peer in peers:
        pl.semaphore_signal(
            barrier, inc=1, device_id={"ctx": peer}, device_id_type=pl.DeviceIdType.MESH
        )

    def copy(number, source, target, device):
        return pltpu.make_async_remote_copy(
            src_ref=source,
            dst_ref=target,
            send_sem=send_sem.at[number],
            recv_sem=recv_sem.at[number],
            device_id={"ctx": device},
            device_id_type=pl.DeviceIdType.MESH,
        )

    for which, ref in ((0, k_ref), (1, v_ref)):
        loads[which].wait()
        for half in range(2):
            c1[which, half * 128:(half + 1) * 128] = pair_mean(ref[half * 256:(half + 1) * 256])
        c2[which] = pair_mean(c1[which])
        c3[which] = pair_mean(c2[which])
        c4[which] = pair_mean(c3[which])
        c5[which] = pair_mean(c4[which])
    c6[...] = pair_mean(c5[...].reshape(32, c5.shape[2]))
    c7[...] = pair_mean(c6[...], 16)

    pl.semaphore_wait(barrier, len(peers))

    side_a, side_b = flip(me, 2), flip(me, 6)
    twin = flip(me, 1)
    copies = {}

    def send(number, source, target, device):
        copies[number] = copy(number, source, target, device)
        copies[number].start()

    send(LEVEL5, c5, far567.at[:, core, x, pl.ds(0, 16)], flip(me, 8))
    for j in range(2):
        send(LEVEL6 + j, c6, got6.at[j], flip(me, 16 + 8 * j))
    for j in range(4):
        send(LEVEL7 + j, c7, got7.at[j], flip(me, 32 + 8 * j))
    send(LEVEL4, c4, far4.at[:, core, 0], side_b)
    head_rows, tail_rows = pl.ds(0, BLOCK), pl.ds(ROWS - BLOCK, BLOCK)
    send(HALO, k_hbm.at[tail_rows], halo.at[0, 0], up)
    send(HALO + 1, v_hbm.at[tail_rows], halo.at[1, 0], up)
    send(HALO + 2, k_hbm.at[head_rows], halo.at[0, 1], down)
    send(HALO + 3, v_hbm.at[head_rows], halo.at[1, 1], down)
    send(LEVEL2, c2, far2, twin)
    send(LEVEL3, c3.at[0], far3.at[0, core], side_a)

    def attend(head, row, rows, keys, values, first=False, last=False, valid=None):
        lanes = pl.ds(pl.multiple_of(head * HEAD_DIM, HEAD_DIM), HEAD_DIM)
        span = pl.ds(row, rows)
        count = keys.shape[0]
        scores = lax.dot_general(
            q_ref[span, lanes], keys, (((1,), (1,)), ((), ())), preferred_element_type=F32
        )
        if valid is not None:
            edge = jnp.where(valid, scores[:, :BLOCK], MASKED)
            scores = jnp.concatenate([edge, scores[:, BLOCK:]], axis=1)
        top = jnp.max(scores, axis=1, keepdims=True)
        if first:
            new = jnp.broadcast_to(top, (rows, 128))
        else:
            old = peak[head, span]
            new = jnp.maximum(old, top)
            fade = jnp.exp2((old - new) * scale)
        wide = jnp.concatenate([new] * (count // 128), axis=1)
        weights = jnp.exp2((scores - wide) * scale).astype(BF16)
        ones = jnp.ones((count, 128), BF16)
        both = jnp.dot(
            weights, jnp.concatenate([values, ones], axis=1), preferred_element_type=F32
        )
        part, part_total = both[:, :128], both[:, 128:]
        if not first:
            part = acc[head, span] * fade + part
            part_total = total[head, span] * fade + part_total
        if last:
            o_ref[span, lanes] = (part / part_total).astype(BF16)
        else:
            acc[head, span] = part
            total[head, span] = part_total
            peak[head, span] = new

    def lanes_of(head):
        return pl.ds(pl.multiple_of(head * HEAD_DIM, HEAD_DIM), HEAD_DIM)

    def own(head, carry):
        lanes = lanes_of(head)
        for block in range(4):
            low, high = max(block - 1, 0) * BLOCK, min(block + 2, 4) * BLOCK
            side = pl.ds(128 if block < 2 else 0, 128)
            keys = jnp.concatenate([k_ref[low:high, lanes], c1[0, side, lanes]], axis=0)
            values = jnp.concatenate([v_ref[low:high, lanes], c1[1, side, lanes]], axis=0)
            attend(head, block * BLOCK, BLOCK, keys, values, first=True)
        return carry

    loads[2].wait()
    lax.fori_loop(0, heads, own, 0)

    for number in range(LEVEL5, LEVEL7 + 4):
        copies[number].wait_recv()
    for which in range(2):
        rows6 = [got6[j, 8 * which:8 * which + 8].astype(F32) for j in range(2)]
        rows7 = [got7[j, 0:8].astype(F32)[4 * which:4 * which + 4] for j in range(4)]
        far567[which, core, x, 16:32] = jnp.concatenate(rows6, axis=0).astype(BF16)
        far567[which, core, x, 32:48] = jnp.concatenate(rows7, axis=0).astype(BF16)
    def pack(place):
        return far567.at[:, core, place]

    send(ALONG_X, pack(x), pack(x), side_a)
    send(ALONG_X + 1, pack(x), pack(x), side_b)
    send(SHARE, pack(x), pack(x), twin)
    copies[LEVEL4].wait_recv()
    send(LEVEL4 + 1, far4.at[:, core, 0], far4.at[:, core, 1], side_a)
    send(SHARE4, far4.at[:, core, 0], far4.at[:, core, 0], twin)
    send(LEVEL3 + 1, c3.at[1], far3.at[1, core], side_a)

    for number in range(HALO, LEVEL2 + 1):
        copies[number].wait_recv()

    def near(head, carry):
        lanes = lanes_of(head)
        keys2, values2 = far2[0, :, lanes], far2[1, :, lanes]
        for side, row, valid in ((0, 0, me > 0), (1, 3 * BLOCK, me < CTX - 1)):
            keys = jnp.concatenate([halo[0, side, :, lanes], keys2], axis=0)
            values = jnp.concatenate([halo[1, side, :, lanes], values2], axis=0)
            attend(head, row, BLOCK, keys, values, valid=valid)
        attend(head, BLOCK, 2 * BLOCK, keys2, values2)
        return carry

    lax.fori_loop(0, heads, near, 0)

    xa, xb, xc = flip(x, 1), flip(x, 3), flip(x, 2)
    copies[ALONG_X].wait_recv()
    send(ALONG_X + 2, pack(xa), pack(xa), side_b)
    send(SHARE + 1, pack(xa), pack(xa), twin)
    copies[ALONG_X + 1].wait_recv()
    send(SHARE + 2, pack(xb), pack(xb), twin)
    copies[LEVEL4 + 1].wait_recv()
    send(SHARE4 + 1, far4.at[:, core, 1], far4.at[:, core, 1], twin)
    copies[ALONG_X + 2].wait_recv()
    send(SHARE + 3, pack(xc), pack(xc), twin)
    for number in (LEVEL3, LEVEL3 + 1):
        copies[number].wait_recv()
    send(SHARE3, far3.at[:, core], far3.at[:, core], twin)
    for number in (SHARE4, SHARE4 + 1, SHARE, SHARE + 1, SHARE + 2, SHARE + 3):
        copies[number].wait_recv()

    def distant(head, carry):
        lanes = lanes_of(head)
        keys, values = (
            jnp.concatenate(
                [
                    far567[which, :, :, :, lanes].reshape(8 * PACK, HEAD_DIM),
                    far4[which, :, :, :, lanes].reshape(128, HEAD_DIM),
                ],
                axis=0,
            )
            for which in range(2)
        )
        for part in range(2):
            attend(head, part * 256, 256, keys, values)
        return carry

    lax.fori_loop(0, heads, distant, 0)

    copies[SHARE3].wait_recv()

    def level3(head, carry):
        lanes = lanes_of(head)
        keys = far3[0, :, :, lanes].reshape(128, HEAD_DIM)
        values = far3[1, :, :, lanes].reshape(128, HEAD_DIM)
        attend(head, 0, ROWS, keys, values, last=True)
        return carry

    lax.fori_loop(0, heads, level3, 0)

    for item in copies.values():
        item.wait_send()


def per_device(queries, keys, values):
    rows, width = queries.shape
    heads = width // HEAD_DIM
    state = pltpu.VMEM((heads, rows, 128), F32)
    return pl.pallas_call(
        kernel,
        out_shape=jax.ShapeDtypeStruct((rows, width), BF16),
        in_specs=[pl.BlockSpec(memory_space=pltpu.HBM)] * 3,
        out_specs=pl.BlockSpec(memory_space=pltpu.VMEM),
        scratch_shapes=[
            pltpu.VMEM((rows, width), BF16),
            pltpu.VMEM((rows, width), BF16),
            pltpu.VMEM((rows, width), BF16),
            pltpu.VMEM((2, 2, BLOCK, width), BF16),
            pltpu.VMEM((2, 256, width), BF16),
            pltpu.VMEM((2, 128, width), BF16),
            pltpu.VMEM((2, 64, width), BF16),
            pltpu.VMEM((2, 32, width), BF16),
            pltpu.VMEM((2, 16, width), BF16),
            pltpu.VMEM((16, width), BF16),
            pltpu.VMEM((16, width), BF16),
            pltpu.VMEM((2, 128, width), BF16),
            pltpu.VMEM((2, 2, 64, width), BF16),
            pltpu.VMEM((2, 2, 2, 32, width), BF16),
            pltpu.VMEM((2, 16, width), BF16),
            pltpu.VMEM((4, 16, width), BF16),
            pltpu.VMEM((2, 2, 4, PACK, width), BF16),
            state, state, state,
            pltpu.SemaphoreType.DMA((COPIES,)),
            pltpu.SemaphoreType.DMA((COPIES,)),
            pltpu.SemaphoreType.DMA((3,)),
        ],
        compiler_params=pltpu.CompilerParams(
            collective_id=0, has_side_effects=True, vmem_limit_bytes=62 * 1024 * 1024
        ),
        name="hierarchical_attention",
    )(queries, keys, values)


def solution(mesh):
    return jax.shard_map(
        per_device,
        mesh=mesh,
        in_specs=(P(("dp", "ctx"), "tp"), P(("dp", "ctx"), "tp"), P(("dp", "ctx"), "tp")),
        out_specs=P(("dp", "ctx"), "tp"),
        check_vma=False,
    )
```

```python
import functools
import math

import jax
import jax.numpy as jnp
from jax import lax
from jax.experimental import pallas as pl
from jax.experimental.pallas import tpu as pltpu
from jax.sharding import PartitionSpec as P

HEAD_DIM = 128
BLOCK = 128
ROWS = 512
CTX = 64
PACK = 48
MASKED = -1.0e30
LOG2E = 1.4426950408889634

F32 = jnp.float32
BF16 = jnp.bfloat16

HALO = 0
LEVEL2 = 4
LEVEL3 = 5
LEVEL4 = 7
LEVEL5 = 9
LEVEL6 = 10
LEVEL7 = 12
ALONG_X = 16
SHARE4 = 19
SHARE3 = 21
SHARE = 22
COPIES = 26


def flip(place, mask):
    bit = 1
    while bit <= mask:
        if mask & bit:
            place = place + bit * (1 - 2 * lax.rem(lax.div(place, bit), 2))
        bit *= 2
    return place


def averaging(rows, cols):
    row = lax.broadcasted_iota(jnp.int32, (rows, cols), 0)
    col = lax.broadcasted_iota(jnp.int32, (rows, cols), 1)
    hit = (col == 2 * row) | (col == 2 * row + 1)
    return jnp.where(hit, 0.5, 0.0).astype(BF16)


def pair_mean(source, rows=None):
    rows = source.shape[0] // 2 if rows is None else rows
    weights = averaging(rows, source.shape[0])
    return jnp.dot(weights, source, preferred_element_type=F32).astype(BF16)


def kernel(
    q_hbm, k_hbm, v_hbm, o_ref, q_ref, k_ref, v_ref,
    halo, c1, c2, c3, c4, c5, c6, c7, far2, far3, far4, got6, got7, far567,
    acc, peak, total, send_sem, recv_sem, load_sem,
):
    heads = q_ref.shape[1] // HEAD_DIM
    scale = LOG2E / math.sqrt(HEAD_DIM)
    me = lax.axis_index("ctx")
    core = lax.rem(me, 2)
    x = lax.rem(lax.div(me, 2), 4)
    up = lax.rem(me + 1, CTX)
    down = lax.rem(me + CTX - 1, CTX)

    loads = [
        pltpu.make_async_copy(source, target, load_sem.at[number])
        for number, (source, target) in enumerate(((k_hbm, k_ref), (v_hbm, v_ref), (q_hbm, q_ref)))
    ]
    for load in loads:
        load.start()

    barrier = pltpu.get_barrier_semaphore()
    peers = [up, down] + [flip(me, mask) for mask in (1, 2, 4, 6, 8, 16, 24, 32, 40, 48, 56)]
    for peer in peers:
        pl.semaphore_signal(
            barrier, inc=1, device_id={"ctx": peer}, device_id_type=pl.DeviceIdType.MESH
        )

    def copy(number, source, target, device):
        return pltpu.make_async_remote_copy(
            src_ref=source,
            dst_ref=target,
            send_sem=send_sem.at[number],
            recv_sem=recv_sem.at[number],
            device_id={"ctx": device},
            device_id_type=pl.DeviceIdType.MESH,
        )

    for which, ref in ((0, k_ref), (1, v_ref)):
        loads[which].wait()
        for half in range(2):
            c1[which, half * 128:(half + 1) * 128] = pair_mean(ref[half * 256:(half + 1) * 256])
        c2[which] = pair_mean(c1[which])
        c3[which] = pair_mean(c2[which])
        c4[which] = pair_mean(c3[which])
        c5[which] = pair_mean(c4[which])
    c6[...] = pair_mean(c5[...].reshape(32, c5.shape[2]))
    c7[...] = pair_mean(c6[...], 16)

    pl.semaphore_wait(barrier, len(peers))

    side_a, side_b = flip(me, 2), flip(me, 6)
    twin = flip(me, 1)
    copies = {}

    def send(number, source, target, device):
        copies[number] = copy(number, source, target, device)
        copies[number].start()

    send(LEVEL5, c5, far567.at[:, core, x, pl.ds(0, 16)], flip(me, 8))
    for j in range(2):
        send(LEVEL6 + j, c6, got6.at[j], flip(me, 16 + 8 * j))
    for j in range(4):
        send(LEVEL7 + j, c7, got7.at[j], flip(me, 32 + 8 * j))
    send(LEVEL4, c4, far4.at[:, core, 0], side_b)
    head_rows, tail_rows = pl.ds(0, BLOCK), pl.ds(ROWS - BLOCK, BLOCK)
    send(HALO, k_hbm.at[tail_rows], halo.at[0, 0], up)
    send(HALO + 1, v_hbm.at[tail_rows], halo.at[1, 0], up)
    send(HALO + 2, k_hbm.at[head_rows], halo.at[0, 1], down)
    send(HALO + 3, v_hbm.at[head_rows], halo.at[1, 1], down)
    send(LEVEL2, c2, far2, twin)

    def attend(head, row, rows, keys, values, first=False, last=False, valid=None):
        lanes = pl.ds(pl.multiple_of(head * HEAD_DIM, HEAD_DIM), HEAD_DIM)
        span = pl.ds(row, rows)
        count = keys.shape[0]
        scores = lax.dot_general(
            q_ref[span, lanes], keys, (((1,), (1,)), ((), ())), preferred_element_type=F32
        )
        if valid is not None:
            edge = jnp.where(valid, scores[:, :BLOCK], MASKED)
            scores = jnp.concatenate([edge, scores[:, BLOCK:]], axis=1)
        top = jnp.max(scores, axis=1, keepdims=True)
        if first:
            new = jnp.broadcast_to(top, (rows, 128))
        else:
            old = peak[head, span]
            new = jnp.maximum(old, top)
            fade = jnp.exp2((old - new) * scale)
        spread = [new] * (count // 128)
        if count % 128:
            spread.append(new[:, :count % 128])
        wide = jnp.concatenate(spread, axis=1)
        weights = jnp.exp2((scores - wide) * scale).astype(BF16)
        ones = jnp.ones((count, 128), BF16)
        both = jnp.dot(
            weights, jnp.concatenate([values, ones], axis=1), preferred_element_type=F32
        )
        part, part_total = both[:, :128], both[:, 128:]
        if not first:
            part = acc[head, span] * fade + part
            part_total = total[head, span] * fade + part_total
        if last:
            o_ref[span, lanes] = (part / part_total).astype(BF16)
        else:
            acc[head, span] = part
            total[head, span] = part_total
            peak[head, span] = new

    def lanes_of(head):
        return pl.ds(pl.multiple_of(head * HEAD_DIM, HEAD_DIM), HEAD_DIM)

    def own(head, carry):
        lanes = lanes_of(head)
        for block in range(4):
            low, high = max(block - 1, 0) * BLOCK, min(block + 2, 4) * BLOCK
            side = pl.ds(128 if block < 2 else 0, 128)
            keys = jnp.concatenate([k_ref[low:high, lanes], c1[0, side, lanes]], axis=0)
            values = jnp.concatenate([v_ref[low:high, lanes], c1[1, side, lanes]], axis=0)
            attend(head, block * BLOCK, BLOCK, keys, values, first=True)
        return carry

    loads[2].wait()
    lax.fori_loop(0, heads // 2, own, 0)
    copies[LEVEL4].wait_recv()
    send(LEVEL4 + 1, far4.at[:, core, 0], far4.at[:, core, 1], side_a)
    send(SHARE4, far4.at[:, core, 0], far4.at[:, core, 0], twin)
    lax.fori_loop(heads // 2, heads, own, 0)

    for number in range(LEVEL5, LEVEL7 + 4):
        copies[number].wait_recv()
    for which in range(2):
        rows6 = [got6[j, 8 * which:8 * which + 8].astype(F32) for j in range(2)]
        rows7 = [got7[j, 0:8].astype(F32)[4 * which:4 * which + 4] for j in range(4)]
        far567[which, core, x, 16:32] = jnp.concatenate(rows6, axis=0).astype(BF16)
        far567[which, core, x, 32:48] = jnp.concatenate(rows7, axis=0).astype(BF16)
    def pack(place):
        return far567.at[:, core, place]

    send(ALONG_X, pack(x), pack(x), side_a)
    send(ALONG_X + 1, pack(x), pack(x), side_b)
    send(SHARE, pack(x), pack(x), twin)
    for which in range(2):
        send(LEVEL3 + which, c3.at[which], far3.at[which, core], side_a)

    for number in range(HALO, LEVEL2 + 1):
        copies[number].wait_recv()

    def near(head, carry):
        lanes = lanes_of(head)
        keys2, values2 = far2[0, :, lanes], far2[1, :, lanes]
        for side, row, valid in ((0, 0, me > 0), (1, 3 * BLOCK, me < CTX - 1)):
            keys = jnp.concatenate([halo[0, side, :, lanes], keys2], axis=0)
            values = jnp.concatenate([halo[1, side, :, lanes], values2], axis=0)
            attend(head, row, BLOCK, keys, values, valid=valid)
        attend(head, BLOCK, 2 * BLOCK, keys2, values2)
        return carry

    lax.fori_loop(0, heads, near, 0)

    xa, xb, xc = flip(x, 1), flip(x, 3), flip(x, 2)
    copies[ALONG_X].wait_recv()
    send(ALONG_X + 2, pack(xa), pack(xa), side_b)
    send(SHARE + 1, pack(xa), pack(xa), twin)
    copies[ALONG_X + 1].wait_recv()
    send(SHARE + 2, pack(xb), pack(xb), twin)
    copies[LEVEL4 + 1].wait_recv()
    send(SHARE4 + 1, far4.at[:, core, 1], far4.at[:, core, 1], twin)
    for number in (SHARE4, SHARE4 + 1, SHARE, SHARE + 1):
        copies[number].wait_recv()

    def pair(place, rest, head, carry):
        lanes = lanes_of(head)
        base = place - lax.rem(place, 2)
        keys, values = (
            jnp.concatenate(
                [source[which, :, :, :, lanes].reshape(128, HEAD_DIM) for source in rest]
                + [far567[which, :, pl.ds(base, 2), :, lanes].reshape(4 * PACK, HEAD_DIM)],
                axis=0,
            )
            for which in range(2)
        )
        for part in range(2):
            attend(head, part * 256, 256, keys, values)
        return carry

    near_pair = functools.partial(pair, x, [far4])
    lax.fori_loop(0, heads * 3 // 4, near_pair, 0)
    copies[ALONG_X + 2].wait_recv()
    send(SHARE + 3, pack(xc), pack(xc), twin)
    lax.fori_loop(heads * 3 // 4, heads, near_pair, 0)

    for number in (LEVEL3, LEVEL3 + 1):
        copies[number].wait_recv()
    send(SHARE3, far3.at[:, core], far3.at[:, core], twin)
    for number in (SHARE + 2, SHARE + 3):
        copies[number].wait_recv()
    lax.fori_loop(0, heads, functools.partial(pair, xc, []), 0)

    copies[SHARE3].wait_recv()

    def level3(head, carry):
        lanes = lanes_of(head)
        keys = far3[0, :, :, lanes].reshape(128, HEAD_DIM)
        values = far3[1, :, :, lanes].reshape(128, HEAD_DIM)
        attend(head, 0, ROWS, keys, values, last=True)
        return carry

    lax.fori_loop(0, heads, level3, 0)

    for item in copies.values():
        item.wait_send()


def per_device(queries, keys, values):
    rows, width = queries.shape
    heads = width // HEAD_DIM
    state = pltpu.VMEM((heads, rows, 128), F32)
    return pl.pallas_call(
        kernel,
        out_shape=jax.ShapeDtypeStruct((rows, width), BF16),
        in_specs=[pl.BlockSpec(memory_space=pltpu.HBM)] * 3,
        out_specs=pl.BlockSpec(memory_space=pltpu.VMEM),
        scratch_shapes=[
            pltpu.VMEM((rows, width), BF16),
            pltpu.VMEM((rows, width), BF16),
            pltpu.VMEM((rows, width), BF16),
            pltpu.VMEM((2, 2, BLOCK, width), BF16),
            pltpu.VMEM((2, 256, width), BF16),
            pltpu.VMEM((2, 128, width), BF16),
            pltpu.VMEM((2, 64, width), BF16),
            pltpu.VMEM((2, 32, width), BF16),
            pltpu.VMEM((2, 16, width), BF16),
            pltpu.VMEM((16, width), BF16),
            pltpu.VMEM((16, width), BF16),
            pltpu.VMEM((2, 128, width), BF16),
            pltpu.VMEM((2, 2, 64, width), BF16),
            pltpu.VMEM((2, 2, 2, 32, width), BF16),
            pltpu.VMEM((2, 16, width), BF16),
            pltpu.VMEM((4, 16, width), BF16),
            pltpu.VMEM((2, 2, 4, PACK, width), BF16),
            state, state, state,
            pltpu.SemaphoreType.DMA((COPIES,)),
            pltpu.SemaphoreType.DMA((COPIES,)),
            pltpu.SemaphoreType.DMA((3,)),
        ],
        compiler_params=pltpu.CompilerParams(
            collective_id=0, has_side_effects=True, vmem_limit_bytes=62 * 1024 * 1024
        ),
        name="hierarchical_attention",
    )(queries, keys, values)


def solution(mesh):
    return jax.shard_map(
        per_device,
        mesh=mesh,
        in_specs=(P(("dp", "ctx"), "tp"), P(("dp", "ctx"), "tp"), P(("dp", "ctx"), "tp")),
        out_specs=P(("dp", "ctx"), "tp"),
        check_vma=False,
    )
```

```python
import math

import jax
import jax.numpy as jnp
from jax import lax
from jax.experimental import pallas as pl
from jax.experimental.pallas import tpu as pltpu
from jax.sharding import PartitionSpec as P

HEAD_DIM = 128
BLOCK = 128
ROWS = 512
CTX = 64
PACK = 48
MASKED = -1.0e30
LOG2E = 1.4426950408889634

F32 = jnp.float32
BF16 = jnp.bfloat16

HALO = 0
LEVEL2 = 4
LEVEL3 = 5
LEVEL4 = 7
LEVEL5 = 9
LEVEL6 = 10
LEVEL7 = 12
ALONG_X = 16
SHARE4 = 19
SHARE3 = 21
SHARE = 22
COPIES = 26


def flip(place, mask):
    bit = 1
    while bit <= mask:
        if mask & bit:
            place = place + bit * (1 - 2 * lax.rem(lax.div(place, bit), 2))
        bit *= 2
    return place


def averaging(rows, cols):
    row = lax.broadcasted_iota(jnp.int32, (rows, cols), 0)
    col = lax.broadcasted_iota(jnp.int32, (rows, cols), 1)
    hit = (col == 2 * row) | (col == 2 * row + 1)
    return jnp.where(hit, 0.5, 0.0).astype(BF16)


def pair_mean(source, rows=None):
    rows = source.shape[0] // 2 if rows is None else rows
    weights = averaging(rows, source.shape[0])
    return jnp.dot(weights, source, preferred_element_type=F32).astype(BF16)


def kernel(
    q_hbm, k_hbm, v_hbm, o_ref, q_ref, k_ref, v_ref,
    halo, c1, c2, c3, c4, c5, c6, c7, far2, far3, far4, got6, got7, far567,
    acc, peak, total, send_sem, recv_sem, load_sem,
):
    heads = q_ref.shape[1] // HEAD_DIM
    scale = LOG2E / math.sqrt(HEAD_DIM)
    me = lax.axis_index("ctx")
    core = lax.rem(me, 2)
    x = lax.rem(lax.div(me, 2), 4)
    up = lax.rem(me + 1, CTX)
    down = lax.rem(me + CTX - 1, CTX)

    loads = [
        pltpu.make_async_copy(source, target, load_sem.at[number])
        for number, (source, target) in enumerate(((k_hbm, k_ref), (v_hbm, v_ref), (q_hbm, q_ref)))
    ]
    for load in loads:
        load.start()

    barrier = pltpu.get_barrier_semaphore()
    peers = [up, down] + [flip(me, mask) for mask in (1, 2, 4, 6, 8, 16, 24, 32, 40, 48, 56)]
    for peer in peers:
        pl.semaphore_signal(
            barrier, inc=1, device_id={"ctx": peer}, device_id_type=pl.DeviceIdType.MESH
        )

    def copy(number, source, target, device):
        return pltpu.make_async_remote_copy(
            src_ref=source,
            dst_ref=target,
            send_sem=send_sem.at[number],
            recv_sem=recv_sem.at[number],
            device_id={"ctx": device},
            device_id_type=pl.DeviceIdType.MESH,
        )

    for which, ref in ((0, k_ref), (1, v_ref)):
        loads[which].wait()
        for half in range(2):
            c1[which, half * 128:(half + 1) * 128] = pair_mean(ref[half * 256:(half + 1) * 256])
        c2[which] = pair_mean(c1[which])
        c3[which] = pair_mean(c2[which])
        c4[which] = pair_mean(c3[which])
        c5[which] = pair_mean(c4[which])
    c6[...] = pair_mean(c5[...].reshape(32, c5.shape[2]))
    c7[...] = pair_mean(c6[...], 16)

    pl.semaphore_wait(barrier, len(peers))

    side_a, side_b = flip(me, 2), flip(me, 6)
    twin = flip(me, 1)
    copies = {}

    def send(number, source, target, device):
        copies[number] = copy(number, source, target, device)
        copies[number].start()

    send(LEVEL5, c5, far567.at[:, core, x, pl.ds(0, 16)], flip(me, 8))
    for j in range(2):
        send(LEVEL6 + j, c6, got6.at[j], flip(me, 16 + 8 * j))
    for j in range(4):
        send(LEVEL7 + j, c7, got7.at[j], flip(me, 32 + 8 * j))
    send(LEVEL4, c4, far4.at[:, core, 0], side_b)
    head_rows, tail_rows = pl.ds(0, BLOCK), pl.ds(ROWS - BLOCK, BLOCK)
    send(HALO, k_hbm.at[tail_rows], halo.at[0, 0], up)
    send(HALO + 1, v_hbm.at[tail_rows], halo.at[1, 0], up)
    send(HALO + 2, k_hbm.at[head_rows], halo.at[0, 1], down)
    send(HALO + 3, v_hbm.at[head_rows], halo.at[1, 1], down)
    send(LEVEL2, c2, far2, twin)
    for which in range(2):
        send(LEVEL3 + which, c3.at[which], far3.at[which, core], side_a)

    def attend(head, row, rows, keys, values, first=False, last=False, valid=None):
        lanes = pl.ds(pl.multiple_of(head * HEAD_DIM, HEAD_DIM), HEAD_DIM)
        span = pl.ds(row, rows)
        count = keys.shape[0]
        scores = lax.dot_general(
            q_ref[span, lanes], keys, (((1,), (1,)), ((), ())), preferred_element_type=F32
        )
        if valid is not None:
            edge = jnp.where(valid, scores[:, :BLOCK], MASKED)
            scores = jnp.concatenate([edge, scores[:, BLOCK:]], axis=1)
        top = jnp.max(scores, axis=1, keepdims=True)
        if first:
            new = jnp.broadcast_to(top, (rows, 128))
        else:
            old = peak[head, span]
            new = jnp.maximum(old, top)
            fade = jnp.exp2((old - new) * scale)
        wide = jnp.concatenate([new] * (count // 128), axis=1)
        weights = jnp.exp2((scores - wide) * scale).astype(BF16)
        ones = jnp.ones((count, 128), BF16)
        both = jnp.dot(
            weights, jnp.concatenate([values, ones], axis=1), preferred_element_type=F32
        )
        part, part_total = both[:, :128], both[:, 128:]
        if not first:
            part = acc[head, span] * fade + part
            part_total = total[head, span] * fade + part_total
        if last:
            o_ref[span, lanes] = (part / part_total).astype(BF16)
        else:
            acc[head, span] = part
            total[head, span] = part_total
            peak[head, span] = new

    def lanes_of(head):
        return pl.ds(pl.multiple_of(head * HEAD_DIM, HEAD_DIM), HEAD_DIM)

    def own(head, carry):
        lanes = lanes_of(head)
        for block in range(4):
            low, high = max(block - 1, 0) * BLOCK, min(block + 2, 4) * BLOCK
            side = pl.ds(128 if block < 2 else 0, 128)
            keys = jnp.concatenate([k_ref[low:high, lanes], c1[0, side, lanes]], axis=0)
            values = jnp.concatenate([v_ref[low:high, lanes], c1[1, side, lanes]], axis=0)
            attend(head, block * BLOCK, BLOCK, keys, values, first=True)
        return carry

    loads[2].wait()
    lax.fori_loop(0, heads // 2, own, 0)
    copies[LEVEL4].wait_recv()
    send(LEVEL4 + 1, far4.at[:, core, 0], far4.at[:, core, 1], side_a)
    send(SHARE4, far4.at[:, core, 0], far4.at[:, core, 0], twin)
    lax.fori_loop(heads // 2, heads, own, 0)

    for number in range(LEVEL5, LEVEL7 + 4):
        copies[number].wait_recv()
    for which in range(2):
        rows6 = [got6[j, 8 * which:8 * which + 8].astype(F32) for j in range(2)]
        rows7 = [got7[j, 0:8].astype(F32)[4 * which:4 * which + 4] for j in range(4)]
        far567[which, core, x, 16:32] = jnp.concatenate(rows6, axis=0).astype(BF16)
        far567[which, core, x, 32:48] = jnp.concatenate(rows7, axis=0).astype(BF16)
    def pack(place):
        return far567.at[:, core, place]

    send(ALONG_X, pack(x), pack(x), side_a)
    send(ALONG_X + 1, pack(x), pack(x), side_b)
    send(SHARE, pack(x), pack(x), twin)

    for number in range(HALO, LEVEL2 + 1):
        copies[number].wait_recv()

    def near(head, carry):
        lanes = lanes_of(head)
        keys2, values2 = far2[0, :, lanes], far2[1, :, lanes]
        for side, row, valid in ((0, 0, me > 0), (1, 3 * BLOCK, me < CTX - 1)):
            keys = jnp.concatenate([halo[0, side, :, lanes], keys2], axis=0)
            values = jnp.concatenate([halo[1, side, :, lanes], values2], axis=0)
            attend(head, row, BLOCK, keys, values, valid=valid)
        attend(head, BLOCK, 2 * BLOCK, keys2, values2)
        return carry

    lax.fori_loop(0, heads, near, 0)

    xa, xb, xc = flip(x, 1), flip(x, 3), flip(x, 2)
    copies[ALONG_X].wait_recv()
    send(ALONG_X + 2, pack(xa), pack(xa), side_b)
    send(SHARE + 1, pack(xa), pack(xa), twin)
    copies[ALONG_X + 1].wait_recv()
    send(SHARE + 2, pack(xb), pack(xb), twin)
    copies[LEVEL4 + 1].wait_recv()
    send(SHARE4 + 1, far4.at[:, core, 1], far4.at[:, core, 1], twin)
    for number in (LEVEL3, LEVEL3 + 1):
        copies[number].wait_recv()
    send(SHARE3, far3.at[:, core], far3.at[:, core], twin)
    for number in (SHARE4, SHARE4 + 1, SHARE3):
        copies[number].wait_recv()

    def middle(head, carry):
        lanes = lanes_of(head)
        keys, values = (
            jnp.concatenate(
                [
                    far3[which, :, :, lanes].reshape(128, HEAD_DIM),
                    far4[which, :, :, :, lanes].reshape(128, HEAD_DIM),
                ],
                axis=0,
            )
            for which in range(2)
        )
        for part in range(2):
            attend(head, part * 256, 256, keys, values)
        return carry

    lax.fori_loop(0, heads // 2, middle, 0)
    copies[ALONG_X + 2].wait_recv()
    send(SHARE + 3, pack(xc), pack(xc), twin)
    lax.fori_loop(heads // 2, heads, middle, 0)

    for number in range(SHARE, SHARE + 4):
        copies[number].wait_recv()

    def distant(head, carry):
        lanes = lanes_of(head)
        keys = far567[0, :, :, :, lanes].reshape(8 * PACK, HEAD_DIM)
        values = far567[1, :, :, :, lanes].reshape(8 * PACK, HEAD_DIM)
        for part in range(2):
            attend(head, part * 256, 256, keys, values, last=True)
        return carry

    lax.fori_loop(0, heads, distant, 0)

    for item in copies.values():
        item.wait_send()


def per_device(queries, keys, values):
    rows, width = queries.shape
    heads = width // HEAD_DIM
    state = pltpu.VMEM((heads, rows, 128), F32)
    return pl.pallas_call(
        kernel,
        out_shape=jax.ShapeDtypeStruct((rows, width), BF16),
        in_specs=[pl.BlockSpec(memory_space=pltpu.HBM)] * 3,
        out_specs=pl.BlockSpec(memory_space=pltpu.VMEM),
        scratch_shapes=[
            pltpu.VMEM((rows, width), BF16),
            pltpu.VMEM((rows, width), BF16),
            pltpu.VMEM((rows, width), BF16),
            pltpu.VMEM((2, 2, BLOCK, width), BF16),
            pltpu.VMEM((2, 256, width), BF16),
            pltpu.VMEM((2, 128, width), BF16),
            pltpu.VMEM((2, 64, width), BF16),
            pltpu.VMEM((2, 32, width), BF16),
            pltpu.VMEM((2, 16, width), BF16),
            pltpu.VMEM((16, width), BF16),
            pltpu.VMEM((16, width), BF16),
            pltpu.VMEM((2, 128, width), BF16),
            pltpu.VMEM((2, 2, 64, width), BF16),
            pltpu.VMEM((2, 2, 2, 32, width), BF16),
            pltpu.VMEM((2, 16, width), BF16),
            pltpu.VMEM((4, 16, width), BF16),
            pltpu.VMEM((2, 2, 4, PACK, width), BF16),
            state, state, state,
            pltpu.SemaphoreType.DMA((COPIES,)),
            pltpu.SemaphoreType.DMA((COPIES,)),
            pltpu.SemaphoreType.DMA((3,)),
        ],
        compiler_params=pltpu.CompilerParams(
            collective_id=0, has_side_effects=True, vmem_limit_bytes=62 * 1024 * 1024
        ),
        name="hierarchical_attention",
    )(queries, keys, values)


def solution(mesh):
    return jax.shard_map(
        per_device,
        mesh=mesh,
        in_specs=(P(("dp", "ctx"), "tp"), P(("dp", "ctx"), "tp"), P(("dp", "ctx"), "tp")),
        out_specs=P(("dp", "ctx"), "tp"),
        check_vma=False,
    )
```
